256 devices in a mesh: head: 4 (over x), page: 64 (over y, z, core).
Axes of the slice: x: 4, y: 4, z: 8, core: 2. Of those that a mesh axis runs over, the one named last changes fastest.
Arguments:
- hidden: bfloat16 [12, 2048], P(None, 'page'), may hold values from -6 to 6
- q_weight: bfloat16 [2048, 3072], P('page', 'head'), may hold values from -0.125 to 0.125
- key_up: bfloat16 [16, 128, 512], P('head'), may hold values from -0.5 to 0.5
- value_up_weight: bfloat16 [16, 512, 128], P('head'), may hold values from -0.25 to 0.25
- out_weight: bfloat16 [2048, 2048], P('head', 'page'), may hold values from -0.125 to 0.125
- cache: bfloat16 [16, 512, 128, 576], P('head', 'page'), may hold values from -360 to 360
- page_table: int32 [16, 512], P('head', 'page'), may hold values from 0 to 511, each once within a row
- seq_pages: int32 [12], replicated, may hold values from 1 to 128, 512 in all
- keep_rows: int32 [16, 512, 64], P('head'), may hold values from 0 to 127, as said below
- fold_mass: bfloat16 [16, 512, 64], P('head'), may hold values from 0.5 to 4
- new_place: int32 [16, 512], P('head'), may hold values from 0 to 2047, as said below
- norm_gain: bfloat16 [2048], replicated, may hold values from 0.099609375 to 1.8984375
- router: bfloat16 [2048, 64], replicated, may hold values from -0.125 to 0.125
- routes: int32 [12, 6], replicated, may hold values from 0 to 63, all different within a row
- w_gate: bfloat16 [64, 2048, 1408], P('page', None, 'head'), may hold values from -0.125 to 0.125
- w_up: bfloat16 [64, 2048, 1408], P('page', None, 'head'), may hold values from -0.125 to 0.125
- w_down: bfloat16 [64, 1408, 2048], P('page', 'head'), may hold values from -0.15625 to 0.15625
Outputs:
- attn_out: bfloat16 [12, 2048], replicated
- moe_out: bfloat16 [12, 2048], replicated
- new_rows: bfloat16 [8192, 64, 576], P(('head', 'page'))
- new_mass: bfloat16 [8192, 64], P(('head', 'page'))
The draws below stay inside these ranges and needn't reach their ends.
Inputs may be any that keep to these rules, and one draw needn't show every extreme that they name: `keep_rows`: the 64 entries of each head and page are distinct. `new_place`: for each group of heads h // 4 the places form a permutation of 0 to 2047. Among the blocks of one head group whose pages share g // 8, at most 1 have places with the same place // 32, and some reach 1.
All inputs are finite; a program needn't handle non-finite values.
Results may differ from the reference program's by a relative error of at most 0.035.
Values may be sent and summed in bfloat16 or wider, within the bound.
A program may use at most 128 MiB of HBM per device.

```python
import math
import jax
import jax.numpy as jnp
import numpy as np
from jax import lax

D = 2048
HEADS = 16
QK_NOPE = 128
QK_ROPE = 64
VALUE_HEAD_WIDTH = 128
KV_RANK = 512
EXPERT_FF = 1408
TOP_K = 6
PAGE_ROWS = 128
KEPT_ROWS = 64
REQUESTS = 12
PAGES_DEV = 8
LATENT = 576
EXPERTS = 64
HEAD_DEV = 4
PAGES = 512
BLOCKS_DEV = 32
MOST_PAGES = 128
N_PAGE = 64


def draw_cache(key, part):
    base_key = jax.random.fold_in(key, 0)
    shape = (HEADS, PAGES, PAGE_ROWS, LATENT)
    values = jax.random.truncated_normal(base_key, -6.0, 6.0, shape, jnp.float32)
    return values.astype(jnp.bfloat16)


def draw_keep_rows(key, part):
    keys = jax.random.split(key, HEADS * PAGES)

    def one_page(one_key):
        return jax.random.permutation(one_key, PAGE_ROWS)[:KEPT_ROWS]
    picked = jax.vmap(one_page)(keys)
    return picked.reshape(HEADS, PAGES, KEPT_ROWS).astype(jnp.int32)


def draw_new_place(key, part):
    group_keys = jax.random.split(key, HEADS // HEAD_DEV)

    def one_group(group_key):
        key_outer, key_inner, key_offset, key_slot = jax.random.split(group_key, 4)
        outer = jax.random.permutation(key_outer, N_PAGE)
        inner = jax.random.permutation(key_inner, N_PAGE)
        start_offsets = jax.random.permutation(key_offset, N_PAGE)
        slots = jax.random.permutation(key_slot, BLOCKS_DEV)
        source = jnp.arange(N_PAGE)[:, None]
        local = jnp.arange(BLOCKS_DEV)[None, :]
        target = outer[(inner[source] + start_offsets[local % N_PAGE]) % N_PAGE]
        places = target * BLOCKS_DEV + slots[local]
        return places.reshape(N_PAGE, HEAD_DEV, PAGES_DEV).transpose(1, 0, 2).reshape(HEAD_DEV, PAGES)
    return jax.vmap(one_group)(group_keys).reshape(HEADS, PAGES).astype(jnp.int32)


def block_levels(stream_key, dims, shards, smallest, top_value):
    loudness = 1.0
    for position, parts in shards:
        heights = jax.random.uniform(jax.random.fold_in(jax.random.fold_in(stream_key, 6), position), (parts,), jnp.float32, smallest / len(shards), top_value / len(shards))
        loudness = loudness * jnp.repeat(jnp.exp(heights), dims[position] // parts).reshape((-1,) + (1,) * (len(dims) - 1 - position))
    return loudness


def different_ones(stream_key, rows, amount, top, lift):
    order = jax.random.permutation(jax.random.fold_in(stream_key, 1), amount)
    pull = order
    for power in range(3):
        pull = pull * pull // amount
    pull = pull * lift // amount
    chance = jax.random.randint(jax.random.fold_in(stream_key, 2), (rows, amount), 0, 4096) + pull
    fixed_rows = jax.random.permutation(jax.random.fold_in(stream_key, 3), rows)[jnp.arange(amount) % rows]
    chance = jnp.where(jnp.arange(rows)[:, None] == fixed_rows[None, :], 1 << 14, chance)
    score = chance * amount + jnp.arange(amount)
    return lax.top_k(score.astype(jnp.int32), top)[1].astype(jnp.int32)


def length_profile(amount, total, limit, lean):
    loads = [(1 << 20) // math.isqrt(standing ** lean) + 1 for standing in range(2, amount + 1)]
    surplus, holding = total - limit - (amount - 1), [1] * (amount - 1)
    while surplus > 0:
        free = [i for i in range(amount - 1) if holding[i] < limit]
        pool, left = sum([loads[i] for i in free]), surplus
        for i in free:
            extra = min(limit - holding[i], max(1, left * loads[i] // pool), surplus)
            holding[i] = holding[i] + extra
            surplus = surplus - extra
    return np.array([limit] + holding)


def ragged_sizes(rng, amount, total, most, lean):
    if amount == 2:
        one = jax.random.randint(rng, (), max(1, total - most), min(most, total - 1) + 1)
        return jnp.stack([one, total - one])
    sizes = jnp.asarray(length_profile(amount, total, most, lean), jnp.int32)
    twos = (amount - 1) // 2
    source_of, receiver = sizes[1:1 + 2 * twos:2], sizes[2:2 + 2 * twos:2]
    room = jnp.minimum(source_of - 1, most - receiver)
    passed = jax.random.randint(jax.random.fold_in(rng, 1), (twos,), 0, 1 << 20) % (room + 1)
    sizes = sizes.at[1:1 + 2 * twos:2].set(source_of - passed).at[2:2 + 2 * twos:2].set(receiver + passed)
    return sizes[jax.random.permutation(jax.random.fold_in(rng, 2), amount)]


def bell_draw(own_key, shape, deviation, most, pieces=(), kind=jnp.bfloat16):
    drawn = jax.random.normal(own_key, shape, jnp.float32) * deviation
    if len(pieces) > 0:
        drawn = block_levels(own_key, shape, pieces, -0.22, 0.18) * drawn
    return jnp.clip(drawn, min=-most, max=most).astype(kind)


def setup_inputs(seed: int = 0) -> dict:
    seeds = jax.random.split(jax.random.key(seed), 18)
    return {
        "hidden": bell_draw(seeds[0], (REQUESTS, D), 1.0, 6.0, ((1, 64),)),
        "q_weight": bell_draw(seeds[1], (D, HEADS * (QK_NOPE + QK_ROPE)), D ** -0.5, 0.125, ((0, 64), (1, 4))),
        "key_up": bell_draw(seeds[2], (HEADS, QK_NOPE, KV_RANK), QK_NOPE ** -0.5, 0.5, ((0, 4),)),
        "value_up_weight": bell_draw(seeds[3], (HEADS, KV_RANK, VALUE_HEAD_WIDTH), KV_RANK ** -0.5, 0.25, ((0, 4),)),
        "out_weight": bell_draw(seeds[4], (HEADS * VALUE_HEAD_WIDTH, D), (HEADS * VALUE_HEAD_WIDTH) ** -0.5, 0.125, ((0, 4), (1, 64))),
        "cache": draw_cache(jax.random.fold_in(seeds[17], 71), 0),
        "page_table": jax.vmap(lambda own: jax.random.permutation(own, PAGES))(jax.random.split(seeds[6], HEADS)).reshape((HEADS, PAGES)).astype(jnp.int32),
        "seq_pages": ragged_sizes(seeds[7], REQUESTS, PAGES, MOST_PAGES, 2).astype(jnp.int32),
        "keep_rows": draw_keep_rows(jax.random.fold_in(seeds[17], 71), 0),
        "fold_mass": jnp.clip(jnp.exp(math.log(4.0) - 2.0794415 * jax.random.uniform(seeds[9], (HEADS, PAGES, KEPT_ROWS), jnp.float32) ** block_levels(seeds[9], (HEADS, PAGES, KEPT_ROWS), ((0, 4),), -0.2, 0.2)), 0.5, 4.0).astype(jnp.bfloat16),
        "new_place": draw_new_place(jax.random.fold_in(seeds[17], 71), 0),
        "norm_gain": jnp.clip(1.0 + 0.18 * jax.random.normal(seeds[11], (D,), jnp.float32), 0.099609375, 1.8984375).astype(jnp.bfloat16),
        "router": bell_draw(seeds[12], (D, EXPERTS), D ** -0.5, 0.125),
        "routes": different_ones(seeds[13], REQUESTS, EXPERTS, TOP_K, 768),
        "w_gate": bell_draw(seeds[14], (EXPERTS, D, EXPERT_FF), D ** -0.5, 0.125, ((0, 64), (2, 4))),
        "w_up": bell_draw(seeds[15], (EXPERTS, D, EXPERT_FF), D ** -0.5, 0.125, ((0, 64), (2, 4))),
        "w_down": bell_draw(seeds[16], (EXPERTS, EXPERT_FF, D), EXPERT_FF ** -0.5, 0.15625, ((0, 64), (1, 4))),
    }


THETA = 50000.0
ROUTE_SCALE = 2.446
NORM_EPS = 1e-06

def rotate_query(values, positions):
    half_dim = values.shape[-1] // 2
    freqs = THETA ** (-2.0 * jnp.arange(half_dim, dtype=jnp.float32) / values.shape[-1])
    angles = positions.astype(jnp.float32)[:, None] * freqs[None, :]
    cosine = jnp.cos(angles)[:, None, :]
    sine_v = jnp.sin(angles)[:, None, :]
    front = values[..., :half_dim]
    back = values[..., half_dim:]
    return jnp.concatenate([front * cosine - back * sine_v, back * cosine + front * sine_v], axis=-1)

def pick_rows(one_page, row_ids):
    return one_page[row_ids]

def reference(hidden, q_weight, key_up, value_up_weight, out_weight, cache, page_table, seq_pages, keep_rows, fold_mass, new_place, norm_gain, router, routes, w_gate, w_up, w_down):
    head_size = QK_NOPE + QK_ROPE
    queries = jnp.dot(hidden, q_weight, preferred_element_type=jnp.float32).reshape(REQUESTS, HEADS, head_size)
    q_nope = queries[..., :QK_NOPE].astype(jnp.bfloat16)
    positions = seq_pages * PAGE_ROWS - 1
    q_rope = rotate_query(queries[..., QK_NOPE:], positions).astype(jnp.bfloat16)
    q_latent = jnp.einsum('rhn,hnk->rhk', q_nope.astype(jnp.float32), key_up.astype(jnp.float32)).astype(jnp.bfloat16)
    q_full = jnp.concatenate([q_latent, q_rope], axis=-1).transpose(1, 0, 2)
    page_ends = jnp.cumsum(seq_pages)
    request_ids = jnp.arange(REQUESTS, dtype=jnp.int32)

    def one_head(inputs):
        head_cache, head_keep, head_mass, head_lookup_table, head_query = inputs
        compact = jax.vmap(pick_rows)(head_cache, head_keep)
        owner = lax.optimization_barrier(jnp.sum((head_lookup_table[:, None] >= page_ends[None, :]).astype(jnp.int32), axis=1))
        in_request = owner[None, :, None] == request_ids[:, None, None]
        rows_wide = compact.astype(jnp.float32)
        scores = jnp.einsum('rk,pjk->rpj', head_query.astype(jnp.float32), rows_wide) * head_size ** (-0.5)
        masked = jnp.where(in_request, scores, -jnp.inf)
        row_max = lax.optimization_barrier(jnp.max(masked, axis=(1, 2)))
        weights = jnp.where(in_request, head_mass.astype(jnp.float32)[None] * jnp.exp(masked - row_max[:, None, None]), 0.0)
        totals = lax.optimization_barrier(jnp.sum(weights, axis=(1, 2)))
        rounded = lax.optimization_barrier(weights.astype(jnp.bfloat16))
        weighted = jnp.einsum('rpj,pjk->rk', rounded.astype(jnp.float32), rows_wide[..., :KV_RANK])
        return ((weighted / totals[:, None]).astype(jnp.bfloat16), compact)
    latent_output, compact_all = lax.map(one_head, (cache, keep_rows, fold_mass, page_table, q_full))
    head_result_rows = jnp.einsum('usj,ujb->sub', latent_output.astype(jnp.float32), value_up_weight.astype(jnp.float32)).astype(jnp.bfloat16)
    head_result_rows = head_result_rows.reshape(REQUESTS, HEADS * VALUE_HEAD_WIDTH)
    attn_out = jnp.dot(head_result_rows, out_weight, preferred_element_type=jnp.float32).astype(jnp.bfloat16)
    attn_wide = attn_out.astype(jnp.float32)
    mean_sq = lax.optimization_barrier(jnp.mean(attn_wide * attn_wide, axis=-1, keepdims=True))
    normed = (attn_wide * lax.rsqrt(mean_sq + NORM_EPS) * norm_gain.astype(jnp.float32)).astype(jnp.bfloat16)
    logits = jnp.dot(normed, router, preferred_element_type=jnp.float32)
    picked = jax.nn.sigmoid(jnp.take_along_axis(logits, routes, axis=1))
    shares = ROUTE_SCALE * picked / lax.optimization_barrier(jnp.sum(picked, axis=1, keepdims=True))
    expert_ids = jnp.arange(EXPERTS, dtype=jnp.int32)
    combine = lax.optimization_barrier(jnp.sum(jnp.where(routes[:, :, None] == expert_ids[None, None, :], shares[:, :, None], 0.0), axis=1))

    def expert_step(carried, layer_in):
        gate_w, up_w, down_w, share = layer_in
        gate_part = jnp.dot(normed, gate_w, preferred_element_type=jnp.float32)
        up_part = jnp.dot(normed, up_w, preferred_element_type=jnp.float32)
        expert_hidden = (jax.nn.silu(gate_part) * up_part).astype(jnp.bfloat16)
        return (carried + share[:, None] * jnp.dot(expert_hidden, down_w, preferred_element_type=jnp.float32), None)
    expert_total, ignored = lax.scan(expert_step, jnp.zeros((REQUESTS, D), jnp.float32), (w_gate, w_up, w_down, combine.T))
    moe_out = expert_total.astype(jnp.bfloat16)
    group_base = jnp.arange(HEADS, dtype=jnp.int32) // HEAD_DEV * (HEAD_DEV * PAGES)
    targets = (group_base[:, None] + new_place).reshape(-1).astype(jnp.int32)
    new_rows = jnp.zeros((HEADS * PAGES, KEPT_ROWS, LATENT), jnp.bfloat16).at[targets].set(compact_all.reshape(-1, KEPT_ROWS, LATENT))
    new_mass = jnp.zeros((HEADS * PAGES, KEPT_ROWS), jnp.bfloat16).at[targets].set(fold_mass.reshape(-1, KEPT_ROWS))
    return (attn_out, moe_out, new_rows, new_mass)
```

```python
import functools

import jax
import jax.numpy as jnp
from jax import lax
from jax.experimental import pallas as pl
from jax.experimental.pallas import tpu as pltpu
from jax.sharding import PartitionSpec as P

QK_NOPE = 128
QK_ROPE = 64
THETA = 50000.0
ROUTE_SCALE = 2.446
NORM_EPS = 1e-06
NEG = -1e30

MESH = pl.DeviceIdType.MESH
F32 = jnp.float32
BF16 = jnp.bfloat16

HERE = 4
PAGES = 8
BLOCKS = HERE * PAGES
ROWS = 128
KEPT = 64
RANK = 512
LATENT = 576
REQ = 12
GROUPS = 64
NX = 4
PACK = (144, 256)


def dot(a, b, dims=(((1,), (0,)), ((), ()))):
    return lax.dot_general(a, b, dims, preferred_element_type=F32)


def compact_kernel(dest_ref, keep_ref, cache_ref, flat_ref, send_ref, pages, packed, in_sem, out_sem):
    def fetch(b):
        return pltpu.make_async_copy(
            cache_ref.at[b // PAGES, b % PAGES], pages.at[b], in_sem.at[b]
        )

    def put(b):
        return pltpu.make_async_copy(packed.at[b], send_ref.at[dest_ref[b]], out_sem.at[b])

    def start(b, carry):
        fetch(b).start()
        return carry

    lax.fori_loop(0, BLOCKS, start, 0)

    def step(b, carry):
        fetch(b).wait()
        row = lax.broadcasted_iota(jnp.int32, (ROWS, KEPT), 0)
        chosen = (row == keep_ref[pl.ds(b, 1), :]).astype(F32).astype(BF16)
        rows = dot(chosen, pages[b], (((0,), (0,)), ((), ())))
        flat_ref[b] = rows.astype(BF16)
        packed[b, 0:64] = rows[:, 0:256].astype(BF16)
        packed[b, 64:128] = rows[:, 256:512].astype(BF16)
        rope = rows[:, 512:576]
        packed[b, 128:144] = jnp.concatenate(
            [rope[16 * g : 16 * g + 16] for g in range(4)], axis=1
        ).astype(BF16)
        put(b).start()
        return carry

    lax.fori_loop(0, BLOCKS, step, 0)

    def finish(b, carry):
        put(b).wait()
        return carry

    lax.fori_loop(0, BLOCKS, finish, 0)


def compact_blocks(dest, keep, cache):
    return pl.pallas_call(
        compact_kernel,
        out_shape=(
            jax.ShapeDtypeStruct((BLOCKS, KEPT, LATENT), BF16),
            jax.ShapeDtypeStruct((GROUPS, *PACK), BF16),
        ),
        in_specs=[
            pl.BlockSpec(memory_space=pltpu.SMEM),
            pl.BlockSpec(memory_space=pltpu.VMEM),
            pl.BlockSpec(memory_space=pl.ANY),
        ],
        out_specs=(pl.BlockSpec(memory_space=pltpu.VMEM), pl.BlockSpec(memory_space=pl.ANY)),
        scratch_shapes=[
            pltpu.VMEM((BLOCKS, ROWS, LATENT), BF16),
            pltpu.VMEM((BLOCKS, *PACK), BF16),
            pltpu.SemaphoreType.DMA((BLOCKS,)),
            pltpu.SemaphoreType.DMA((BLOCKS,)),
        ],
        compiler_params=pltpu.CompilerParams(vmem_limit_bytes=24 << 20),
        name="compact_blocks",
    )(dest, keep, cache)


def place_kernel(src_ref, recv_ref, rows_ref, held, in_sem):
    def fetch(q):
        return pltpu.make_async_copy(recv_ref.at[src_ref[q]], held.at[q], in_sem.at[q])

    def start(q, carry):
        fetch(q).start()
        return carry

    lax.fori_loop(0, BLOCKS, start, 0)

    def step(q, carry):
        fetch(q).wait()
        rows_ref[q, :, 0:256] = held[q, 0:64]
        rows_ref[q, :, 256:512] = held[q, 64:128]
        rope = held[q, 128:144].astype(F32)
        rows_ref[q, :, 512:576] = jnp.concatenate(
            [rope[:, 64 * g : 64 * g + 64] for g in range(4)], axis=0
        ).astype(BF16)
        return carry

    lax.fori_loop(0, BLOCKS, step, 0)


def place_blocks(src, recv):
    return pl.pallas_call(
        place_kernel,
        out_shape=jax.ShapeDtypeStruct((BLOCKS, KEPT, LATENT), BF16),
        in_specs=[pl.BlockSpec(memory_space=pltpu.SMEM), pl.BlockSpec(memory_space=pl.ANY)],
        out_specs=pl.BlockSpec(memory_space=pltpu.VMEM),
        scratch_shapes=[pltpu.VMEM((BLOCKS, *PACK), BF16), pltpu.SemaphoreType.DMA((BLOCKS,))],
        compiler_params=pltpu.CompilerParams(vmem_limit_bytes=16 << 20),
        name="place_blocks",
    )(src, recv)


OFFSETS = [
    (dy, sign * dz, dc)
    for dz in range(5)
    for dy in range(4)
    for dc in range(2)
    for sign in ((1,) if dz in (0, 4) else (1, -1))
    if (dy, dz, dc) != (0, 0, 0)
]
FEED = (2,) * 13


def split3(v):
    a = v.astype(BF16)
    rest = v - a.astype(F32)
    b = rest.astype(BF16)
    return a, b, (rest - b.astype(F32)).astype(BF16)


def decode_kernel(
    hidden_ref,
    qw_ref,
    owner_ref,
    mass_ref,
    cos_ref,
    sin_ref,
    gain_ref,
    routes_ref,
    key_hbm,
    value_hbm,
    out_hbm,
    flat_hbm,
    router_hbm,
    gate_hbm,
    up_hbm,
    down_hbm,
    send_ref,
    attn_ref,
    moe_ref,
    recv_ref,
    key_v,
    value_v,
    outw_v,
    flat_v,
    router_v,
    gate_v,
    up_v,
    down_v,
    q_out,
    q_in,
    q2_out,
    q2_in,
    q3_out,
    q3_in,
    a_out,
    a_in,
    b_out,
    b_in,
    c_out,
    c_in,
    d_out,
    d_in,
    d2_out,
    d2_in,
    d3_out,
    d3_in,
    e_out,
    e_in,
    e2_out,
    e2_in,
    e3_out,
    e3_in,
    e4_out,
    e4_in,
    load_sem,
    own_sem,
    small_send,
    small_recv,
    bulk_send,
    bulk_recv,
):
    x = lax.axis_index("head")
    p = lax.axis_index("page")
    y, z, c = p // 16, (p // 2) % 8, p % 2
    a = y * 2 + c

    loads = [
        pltpu.make_async_copy(src, dst, load_sem.at[n])
        for n, (src, dst) in enumerate(
            (
                (key_hbm, key_v),
                (flat_hbm, flat_v),
                (value_hbm, value_v),
                (out_hbm, outw_v),
                (router_hbm, router_v),
                (gate_hbm.at[0], gate_v),
                (up_hbm.at[0], up_v),
                (down_hbm.at[0], down_v),
            )
        )
    ]
    for load in loads:
        load.start()
    own = pltpu.make_async_copy(send_ref.at[p], recv_ref.at[p], own_sem)
    own.start()

    barrier = pltpu.get_barrier_semaphore()

    def greet(k, carry):
        pl.semaphore_signal(
            barrier, inc=1, device_id=(x, (p + k) % GROUPS), device_id_type=MESH
        )
        return carry

    lax.fori_loop(1, GROUPS, greet, 0)
    for k in range(1, NX):
        pl.semaphore_signal(barrier, inc=1, device_id=((x + k) % NX, p), device_id_type=MESH)

    part = dot(hidden_ref[...], qw_ref[...])
    width = QK_NOPE + QK_ROPE
    for h in range(HERE):
        q_out[h] = part[:, width * h : width * h + QK_NOPE]
    for n in range(2):
        q_out[HERE + n] = jnp.concatenate(
            [
                part[:, width * h + QK_NOPE : width * (h + 1)]
                for h in (2 * n, 2 * n + 1)
            ],
            axis=1,
        )
    q_out[6] = jnp.zeros_like(q_out[6])
    q_out[7] = jnp.zeros_like(q_out[7])

    pl.semaphore_wait(barrier, GROUPS - 1 + NX - 1)

    fed = []

    def bulk(offset):
        dy, dz, dc = offset
        n = OFFSETS.index(offset)
        to = ((y + dy) % 4) * 16 + ((z + dz + 8) % 8) * 2 + (c + dc) % 2
        return pltpu.make_async_remote_copy(
            send_ref.at[to],
            recv_ref.at[p],
            bulk_send.at[n],
            bulk_recv.at[n],
            device_id=(x, to),
            device_id_type=MESH,
        )

    def feed(count):
        for offset in OFFSETS[len(fed) : len(fed) + count]:
            bulk(offset).start()
            fed.append(offset)

    smalls = []

    def exchange(stage, kind, out, into, scatter):
        copies = []
        size = NX if kind == "x" else 8
        me = {"a": a, "z": z, "x": x}[kind]
        for k in range(1, size):
            other = (me + k) % size
            if kind == "a":
                target = (x, (other // 2) * 16 + z * 2 + other % 2)
            elif kind == "z":
                target = (x, y * 16 + other * 2 + c)
            else:
                target = (other, p)
            copies.append(
                pltpu.make_async_remote_copy(
                    out.at[other] if scatter else out,
                    into.at[me],
                    small_send.at[stage, k],
                    small_recv.at[stage, k],
                    device_id=target,
                    device_id_type=MESH,
                )
            )
        for copy in copies:
            copy.start()
        into[me] = out[me] if scatter else out[...]
        feed(FEED[stage])
        for copy in copies:
            copy.wait_recv()
        smalls.extend(copies)

    def added(into, size):
        total = into[0].astype(F32)
        for n in range(1, size):
            total = total + into[n].astype(F32)
        return total

    exchange(0, "a", q_out, q_in, True)
    q2_out[...] = added(q_in, 8)
    exchange(1, "z", q2_out, q2_in, False)
    mine = added(q2_in, 8)
    lane = lax.broadcasted_iota(jnp.int32, mine.shape, 1)
    turned = jnp.where(lane % 64 < 32, pltpu.roll(mine, 96, 1), pltpu.roll(mine, 32, 1))
    rotated = mine * cos_ref[...] + turned * sin_ref[...]
    q3_out[...] = jnp.where(a < HERE, mine, rotated).astype(BF16)
    exchange(2, "a", q3_out, q3_in, False)

    loads[0].wait()
    loads[1].wait()
    scale = width ** (-0.5)
    rows_here = PAGES * KEPT
    request = lax.broadcasted_iota(jnp.int32, (REQ, rows_here), 0)
    for h in range(HERE):
        rope = q3_in[HERE + h // 2][:, 64 * (h % 2) : 64 * (h % 2) + 64]
        latent_query = dot(q3_in[h], key_v[h]).astype(BF16)
        block = flat_v[h]
        nt = (((1,), (1,)), ((), ()))
        scores = (dot(latent_query, block[:, :RANK], nt) + dot(rope, block[:, RANK:], nt)) * scale
        mine_here = owner_ref[h : h + 1, :] == request
        best = jnp.max(jnp.where(mine_here, scores, NEG), axis=1, keepdims=True)
        weights = jnp.where(mine_here, mass_ref[h : h + 1, :] * jnp.exp(scores - best), 0.0)
        total = jnp.sum(weights, axis=1, keepdims=True)
        summed = dot(weights.astype(BF16), block[:, :RANK])
        stats = jnp.concatenate(
            [
                jnp.broadcast_to(v.astype(F32), (REQ, 16))
                for v in (*split3(best), *split3(total))
            ]
            + [jnp.zeros((REQ, 32), F32)],
            axis=1,
        ).astype(BF16)
        for half in range(2):
            a_out[2 * h + half, :, 0:256] = summed[:, 256 * half : 256 * half + 256].astype(BF16)
            a_out[2 * h + half, :, 256:384] = stats

    def merged(into):
        def stat(n, first):
            return sum(
                into[n, :, 256 + 16 * s : 256 + 16 * s + 16].astype(F32)[:, 0:1]
                for s in range(first, first + 3)
            )

        bests = [stat(n, 0) for n in range(8)]
        best = functools.reduce(jnp.maximum, bests)
        total = jnp.zeros((REQ, 1), F32)
        latent = jnp.zeros((REQ, 256), F32)
        for n in range(8):
            factor = jnp.exp(bests[n] - best)
            total = total + factor * stat(n, 3)
            latent = latent + factor * into[n, :, 0:256].astype(F32)
        return best, total, latent

    exchange(3, "a", a_out, a_in, True)
    best, total, latent = merged(a_in)
    b_out[:, 0:256] = latent.astype(BF16)
    b_out[:, 256:384] = jnp.concatenate(
        [jnp.broadcast_to(v.astype(F32), (REQ, 16)) for v in (*split3(best), *split3(total))]
        + [jnp.zeros((REQ, 32), F32)],
        axis=1,
    ).astype(BF16)
    exchange(4, "z", b_out, b_in, False)
    _, total, latent = merged(b_in)
    latent_out = (latent / total).astype(BF16)
    loads[2].wait()
    c_out[...] = dot(latent_out, value_v[a // 2, pl.ds((a % 2) * 256, 256), :])
    exchange(5, "a", c_out, c_in, False)

    loads[3].wait()
    cols = jnp.zeros((REQ, 32), F32)
    for h in range(HERE):
        head_out = (c_in[2 * h] + c_in[2 * h + 1]).astype(BF16)
        cols = cols + dot(head_out, outw_v[128 * h : 128 * h + 128, :])
    spread = jnp.concatenate([cols] * 4, axis=1)
    lane = lax.broadcasted_iota(jnp.int32, spread.shape, 1)
    d_out[...] = jnp.where(lane // 32 == p % 4, spread, 0.0)
    exchange(6, "x", d_out, d_in, False)
    d2_out[...] = added(d_in, NX).astype(BF16)
    exchange(7, "z", d2_out, d2_in, False)
    for n in range(4):
        d3_out[n] = (d2_in[2 * n].astype(F32) + d2_in[2 * n + 1].astype(F32)).astype(BF16)
    exchange(8, "a", d3_out, d3_in, False)

    tiles = [
        d3_in[2 * (t // 4), t % 4].astype(F32) + d3_in[2 * (t // 4) + 1, t % 4].astype(F32)
        for t in range(16)
    ]
    square = jnp.zeros((REQ, 128), F32)
    for t in range(16):
        attn_ref[:, 128 * t : 128 * t + 128] = tiles[t].astype(BF16)
        square = square + tiles[t] * tiles[t]
    mean = jnp.sum(square, axis=1, keepdims=True) * (1.0 / 2048)
    inverse = lax.rsqrt(mean + NORM_EPS)
    normed = jnp.concatenate(
        [
            (tiles[t] * inverse * gain_ref[:, 128 * t : 128 * t + 128].astype(F32)).astype(BF16)
            for t in range(16)
        ],
        axis=1,
    )

    loads[4].wait()
    logits = dot(normed, router_v[...])
    chance = 1.0 / (1.0 + jnp.exp(-logits))
    expert = lax.broadcasted_iota(jnp.int32, chance.shape, 1)
    routed = jnp.zeros(chance.shape, F32)
    for t in range(routes_ref.shape[1]):
        routed = jnp.where(routes_ref[:, t : t + 1] == expert, 1.0, routed)
    chosen = routed * chance
    share = ROUTE_SCALE * chosen / jnp.sum(chosen, axis=1, keepdims=True)
    share_here = jnp.sum(jnp.where(expert == p, share, 0.0), axis=1, keepdims=True)
    loads[5].wait()
    gate = dot(normed, gate_v[...])
    loads[6].wait()
    up = dot(normed, up_v[...])
    expert_hidden = (gate / (1.0 + jnp.exp(-gate)) * up).astype(BF16)
    loads[7].wait()
    for n in range(8):
        e_out[n] = (
            share_here * dot(expert_hidden, down_v[:, 256 * n : 256 * n + 256])
        ).astype(BF16)
    exchange(9, "a", e_out, e_in, True)
    e2_out[...] = added(e_in, 8).astype(BF16)
    exchange(10, "z", e2_out, e2_in, False)
    e3_out[...] = added(e2_in, 8).astype(BF16)
    exchange(11, "x", e3_out, e3_in, False)
    e4_out[...] = added(e3_in, NX).astype(BF16)
    exchange(12, "a", e4_out, e4_in, False)
    for n in range(8):
        moe_ref[:, 256 * n : 256 * n + 256] = e4_in[n]

    feed(len(OFFSETS))
    for copy in smalls:
        copy.wait_send()
    own.wait()
    for offset in OFFSETS:
        bulk(offset).wait()


def decode(*operands):
    big = [pl.BlockSpec(memory_space=pl.ANY)] * 9
    small = [pl.BlockSpec(memory_space=pltpu.VMEM)] * 8
    tile = (REQ, 128)
    wide = (REQ, 256)
    stat = (REQ, 384)

    def pair(shape, parts, dtype, scatter):
        return [
            pltpu.VMEM((parts, *shape) if scatter else shape, dtype),
            pltpu.VMEM((parts, *shape), dtype),
        ]

    return pl.pallas_call(
        decode_kernel,
        out_shape=(
            jax.ShapeDtypeStruct((REQ, 2048), BF16),
            jax.ShapeDtypeStruct((REQ, 2048), BF16),
            jax.ShapeDtypeStruct((GROUPS, *PACK), BF16),
        ),
        in_specs=small + big,
        out_specs=(
            pl.BlockSpec(memory_space=pltpu.VMEM),
            pl.BlockSpec(memory_space=pltpu.VMEM),
            pl.BlockSpec(memory_space=pl.ANY),
        ),
        scratch_shapes=[
            pltpu.VMEM((HERE, QK_NOPE, RANK), BF16),
            pltpu.VMEM((HERE, RANK, 128), BF16),
            pltpu.VMEM((512, 32), BF16),
            pltpu.VMEM((HERE, PAGES * KEPT, LATENT), BF16),
            pltpu.VMEM((2048, 64), BF16),
            pltpu.VMEM((2048, 352), BF16),
            pltpu.VMEM((2048, 352), BF16),
            pltpu.VMEM((352, 2048), BF16),
            *pair(tile, 8, F32, True),
            *pair(tile, 8, F32, False),
            *pair(tile, 8, BF16, False),
            *pair(stat, 8, BF16, True),
            *pair(stat, 8, BF16, False),
            *pair(tile, 8, F32, False),
            *pair(tile, NX, F32, False),
            *pair(tile, 8, BF16, False),
            *pair((4, *tile), 8, BF16, False),
            *pair(wide, 8, BF16, True),
            *pair(wide, 8, BF16, False),
            *pair(wide, NX, BF16, False),
            *pair(wide, 8, BF16, False),
            pltpu.SemaphoreType.DMA((8,)),
            pltpu.SemaphoreType.DMA,
            pltpu.SemaphoreType.DMA((13, 8)),
            pltpu.SemaphoreType.DMA((13, 8)),
            pltpu.SemaphoreType.DMA((GROUPS,)),
            pltpu.SemaphoreType.DMA((GROUPS,)),
        ],
        compiler_params=pltpu.CompilerParams(
            collective_id=0, has_side_effects=True, vmem_limit_bytes=40 << 20
        ),
        name="decode",
    )(*operands)


def shards(
    hidden,
    q_weight,
    key_up,
    value_up_weight,
    out_weight,
    cache,
    page_table,
    seq_pages,
    keep_rows,
    fold_mass,
    new_place,
    norm_gain,
    router,
    routes,
    w_gate,
    w_up,
    w_down,
):
    page_index = lax.axis_index("page")
    first_page = page_index * PAGES

    def here(array):
        return lax.dynamic_slice_in_dim(array, first_page, PAGES, 1)

    dest = here(new_place).reshape(BLOCKS) // BLOCKS
    keep = here(keep_rows).reshape(BLOCKS, KEPT)
    flat, send = compact_blocks(dest, keep, cache)

    page_ends = jnp.cumsum(seq_pages)
    owner = jnp.sum((page_table[..., None] >= page_ends).astype(jnp.int32), axis=-1)
    row_owner = jnp.repeat(owner, KEPT, axis=1)
    row_mass = here(fold_mass).reshape(HERE, PAGES * KEPT).astype(F32)
    positions = seq_pages * ROWS - 1
    half = QK_ROPE // 2
    freqs = THETA ** (-2.0 * jnp.arange(half, dtype=F32) / QK_ROPE)
    angles = positions.astype(F32)[:, None] * freqs[None, :]
    cosine = jnp.tile(jnp.cos(angles), (1, 4))
    sine = jnp.sin(angles)
    sine = jnp.concatenate([-sine, sine, -sine, sine], axis=1)

    attn_out, moe_out, recv = decode(
        hidden,
        q_weight,
        row_owner,
        row_mass,
        cosine,
        sine,
        norm_gain.reshape(1, -1),
        routes,
        key_up,
        value_up_weight,
        out_weight,
        flat.reshape(HERE, PAGES * KEPT, LATENT),
        router,
        w_gate,
        w_up,
        w_down,
        send,
    )

    slots = page_index * BLOCKS + jnp.arange(BLOCKS, dtype=jnp.int32)
    owned = slots[:, None] == new_place.reshape(1, -1)
    source = jnp.arange(GROUPS * PAGES, dtype=jnp.int32) // PAGES
    src = jnp.sum(jnp.where(owned, jnp.tile(source, HERE)[None, :], 0), axis=1)
    new_mass = jnp.dot(
        owned.astype(BF16), fold_mass.reshape(-1, KEPT), preferred_element_type=F32
    ).astype(BF16)
    new_rows = place_blocks(src, recv)
    return (attn_out, moe_out, new_rows, new_mass)


def solution(mesh):
    in_specs = (
        P(None, "page"),
        P("page", "head"),
        P("head", None, None),
        P("head", None, None),
        P("head", "page"),
        P("head", "page", None, None),
        P("head", "page"),
        P(),
        P("head", None, None),
        P("head", None, None),
        P("head", None),
        P(),
        P(),
        P(),
        P("page", None, "head"),
        P("page", None, "head"),
        P("page", "head", None),
    )
    out_specs = (P(), P(), P(("head", "page"), None, None), P(("head", "page"), None))
    return jax.shard_map(shards, mesh=mesh, in_specs=in_specs, out_specs=out_specs, check_vma=False)
```

```python
import functools

import jax
import jax.numpy as jnp
import numpy as np
from jax import lax
from jax.experimental import pallas as pl
from jax.experimental.pallas import tpu as pltpu
from jax.sharding import PartitionSpec as P

QK_NOPE = 128
QK_ROPE = 64
THETA = 50000.0
ROUTE_SCALE = 2.446
NORM_EPS = 1e-06
NEG = -1e30

MESH = pl.DeviceIdType.MESH
F32 = jnp.float32
BF16 = jnp.bfloat16

HERE = 4
PAGES = 8
BLOCKS = HERE * PAGES
ROWS = 128
KEPT = 64
RANK = 512
LATENT = 576
REQ = 12
GROUPS = 64
NX = 4
PACK = (144, 256)


def dot(a, b, dims=(((1,), (0,)), ((), ()))):
    return lax.dot_general(a, b, dims, preferred_element_type=F32)


NT = (((1,), (1,)), ((), ()))

OFFSETS = [
    (dy, sign * dz, dc)
    for dy in range(4)
    for dc in range(2)
    for dz in range(5)
    for sign in ((1,) if dz in (0, 4) else (1, -1))
    if (dy, dz, dc) != (0, 0, 0)
]
FEED = (0, 5, 5, 6, 5, 5, 5, 5, 5, 5, 5, 5, 5)


def split3(v):
    a = v.astype(BF16)
    rest = v - a.astype(F32)
    b = rest.astype(BF16)
    return a, b, (rest - b.astype(F32)).astype(BF16)


def lane_sum(v):
    total = v[:, 0:128]
    for n in range(1, v.shape[1] // 128):
        total = total + v[:, 128 * n : 128 * n + 128]
    for step in (64, 32, 16, 8, 4, 2, 1):
        total = total + pltpu.roll(total, step, 1)
    return total


def decode_kernel(
    seq_ref,
    table_ref,
    routes_ref,
    hidden_ref,
    qw_ref,
    place_ref,
    freq_ref,
    gain_ref,
    cache_hbm,
    keep_hbm,
    mass_hbm,
    key_hbm,
    value_hbm,
    out_hbm,
    router_hbm,
    gate_hbm,
    up_hbm,
    down_hbm,
    attn_ref,
    moe_ref,
    rows_ref,
    newmass_ref,
    pages,
    keep_v,
    mass_v,
    key_v,
    value_v,
    outw_v,
    router_v,
    gate_v,
    up_v,
    down_v,
    flat_v,
    packed,
    send_v,
    recv_v,
    index_v,
    index_s,
    q_out,
    q_in,
    q2_out,
    q2_in,
    q3_out,
    q3_in,
    a_out,
    a_in,
    b_out,
    b_in,
    c_out,
    c_in,
    d_out,
    d_in,
    d2_out,
    d2_in,
    d3_out,
    d3_in,
    e_out,
    e_in,
    e2_out,
    e2_in,
    e3_out,
    e3_in,
    e4_out,
    e4_in,
    load_sem,
    page_sem,
    index_sem,
    small_send,
    small_recv,
    bulk_send,
    bulk_recv,
):
    x = lax.axis_index("head")
    p = lax.axis_index("page")
    y, z, c = p // 16, (p // 2) % 8, p % 2
    a = y * 2 + c

    barrier = pltpu.get_barrier_semaphore()

    def greet(k, carry):
        pl.semaphore_signal(
            barrier, inc=1, device_id=(x, (p + k) % GROUPS), device_id_type=MESH
        )
        return carry

    lax.fori_loop(1, GROUPS, greet, 0)
    for k in range(1, NX):
        pl.semaphore_signal(barrier, inc=1, device_id=((x + k) % NX, p), device_id_type=MESH)

    keep_load = pltpu.make_async_copy(keep_hbm, keep_v, load_sem.at[0])
    keep_load.start()
    page_loads = [
        pltpu.make_async_copy(cache_hbm.at[h], pages.at[h], page_sem.at[h]) for h in range(HERE)
    ]
    for load in page_loads:
        load.start()
    loads = [
        pltpu.make_async_copy(src, dst, load_sem.at[n + 1])
        for n, (src, dst) in enumerate(
            (
                (key_hbm, key_v),
                (mass_hbm, mass_v),
                (value_hbm, value_v),
                (out_hbm, outw_v),
                (router_hbm, router_v),
                (gate_hbm.at[0], gate_v),
                (up_hbm.at[0], up_v),
                (down_hbm.at[0], down_v),
            )
        )
    ]
    for load in loads:
        load.start()

    lanes = GROUPS * PAGES
    for_device = jnp.zeros((GROUPS, lanes), jnp.int32)
    for_place = jnp.zeros((BLOCKS, lanes), jnp.int32)
    device = lax.broadcasted_iota(jnp.int32, (GROUPS, lanes), 0)
    place = lax.broadcasted_iota(jnp.int32, (BLOCKS, lanes), 0) + p * BLOCKS
    page = lax.broadcasted_iota(jnp.int32, (1, lanes), 1)
    for h in range(HERE):
        row = place_ref[h : h + 1, :]
        target = jnp.where(page // PAGES == p, row // BLOCKS, -1)
        for_device = jnp.where(target == device, h * PAGES + page % PAGES, for_device)
        for_place = jnp.where(row == place, page // PAGES, for_place)
    index_v[0:GROUPS] = jnp.minimum(lane_sum(for_device), BLOCKS - 1)
    index_v[GROUPS:] = jnp.minimum(lane_sum(for_place), GROUPS - 1)
    index_load = pltpu.make_async_copy(index_v, index_s, index_sem)
    index_load.start()

    part = dot(hidden_ref[...], qw_ref[...])
    width = QK_NOPE + QK_ROPE
    for h in range(HERE):
        q_out[h] = part[:, width * h : width * h + QK_NOPE]
    for n in range(2):
        q_out[HERE + n] = jnp.concatenate(
            [part[:, width * h + QK_NOPE : width * (h + 1)] for h in (2 * n, 2 * n + 1)],
            axis=1,
        )
    q_out[6] = jnp.zeros_like(q_out[6])
    q_out[7] = jnp.zeros_like(q_out[7])

    mine_pages = (
        lax.broadcasted_iota(jnp.int32, (PAGES, lanes), 1)
        == lax.broadcasted_iota(jnp.int32, (PAGES, lanes), 0) + p * PAGES
    )
    picker = mine_pages.astype(F32).astype(BF16)
    lane_row = lax.broadcasted_iota(jnp.int32, (KEPT, ROWS), 1).astype(F32)

    def compact(h):
        page_loads[h].wait()
        kept = dot(keep_v[h].astype(F32).astype(BF16), picker, NT)
        for g in range(PAGES):
            chosen = (kept[:, g : g + 1] == lane_row).astype(F32).astype(BF16)
            rows = dot(chosen, pages[h, g], NT)
            block = h * PAGES + g
            flat_v[h, KEPT * g : KEPT * g + KEPT, :] = rows.astype(BF16)
            packed[block, 0:64] = rows[:, 0:256].astype(BF16)
            packed[block, 64:128] = rows[:, 256:512].astype(BF16)
            rope = rows[:, 512:576]
            packed[block, 128:144] = jnp.concatenate(
                [rope[16 * n : 16 * n + 16] for n in range(4)], axis=1
            ).astype(BF16)

    keep_load.wait()
    compact(0)
    compact(1)
    index_load.wait()

    pl.semaphore_wait(barrier, GROUPS - 1 + NX - 1)

    fed = []

    def bulk(offset):
        dy, dz, dc = offset
        n = OFFSETS.index(offset)
        to = ((y + dy) % 4) * 16 + ((z + dz + 8) % 8) * 2 + (c + dc) % 2
        return to, pltpu.make_async_remote_copy(
            send_v.at[n],
            recv_v.at[p],
            bulk_send.at[n],
            bulk_recv.at[n],
            device_id=(x, to),
            device_id_type=MESH,
        )

    def feed(count):
        for offset in OFFSETS[len(fed) : len(fed) + count]:
            to, copy = bulk(offset)
            send_v[len(fed)] = packed[index_s[to, 0]]
            copy.start()
            fed.append(copy)

    smalls = []

    def exchange(stage, kind, out, into, scatter, meanwhile=None):
        copies = []
        size = NX if kind == "x" else 8
        me = {"a": a, "z": z, "x": x}[kind]
        for k in range(1, size):
            other = (me + k) % size
            if kind == "a":
                target = (x, (other // 2) * 16 + z * 2 + other % 2)
            elif kind == "z":
                target = (x, y * 16 + other * 2 + c)
            else:
                target = (other, p)
            copies.append(
                pltpu.make_async_remote_copy(
                    out.at[other] if scatter else out,
                    into.at[me],
                    small_send.at[stage, k],
                    small_recv.at[stage, k],
                    device_id=target,
                    device_id_type=MESH,
                )
            )
        for copy in copies:
            copy.start()
        into[me] = out[me] if scatter else out[...]
        if meanwhile is not None:
            meanwhile()
        feed(FEED[stage])
        for copy in copies:
            copy.wait_recv()
        smalls.extend(copies)

    def added(into, size):
        total = into[0].astype(F32)
        for n in range(1, size):
            total = total + into[n].astype(F32)
        return total

    def compact_rest():
        compact(2)
        compact(3)

    exchange(0, "a", q_out, q_in, True, compact_rest)
    recv_v[p] = packed[index_s[p, 0]]
    q2_out[...] = added(q_in, 8)
    exchange(1, "z", q2_out, q2_in, False)
    mine = added(q2_in, 8)
    request = lax.broadcasted_iota(jnp.int32, mine.shape, 0)
    lane = lax.broadcasted_iota(jnp.int32, mine.shape, 1)
    position = jnp.zeros(mine.shape, jnp.int32)
    for r in range(REQ):
        position = jnp.where(request == r, seq_ref[r] * ROWS - 1, position)
    angle = position.astype(F32) * freq_ref[...]
    first = lane % 64 < 32
    turned = jnp.where(first, -pltpu.roll(mine, 96, 1), pltpu.roll(mine, 32, 1))
    rotated = mine * jnp.cos(angle) + turned * jnp.sin(angle)
    q3_out[...] = jnp.where(a < HERE, mine, rotated).astype(BF16)
    exchange(2, "a", q3_out, q3_in, False)

    loads[0].wait()
    loads[1].wait()
    scale = width ** (-0.5)
    rows_here = PAGES * KEPT
    request = lax.broadcasted_iota(jnp.int32, (REQ, rows_here), 0)
    page = lax.broadcasted_iota(jnp.int32, (1, rows_here), 1) // KEPT
    ends = [seq_ref[0]]
    for r in range(1, REQ):
        ends.append(ends[-1] + seq_ref[r])

    def stats_of(best, total):
        return jnp.concatenate(
            [jnp.broadcast_to(v.astype(F32), (REQ, 16)) for v in (*split3(best), *split3(total))]
            + [jnp.zeros((REQ, 32), F32)],
            axis=1,
        ).astype(BF16)

    for h in range(HERE):
        logical = jnp.zeros((1, rows_here), jnp.int32)
        for g in range(PAGES):
            logical = jnp.where(page == g, table_ref[h, g], logical)
        owner = jnp.zeros((1, rows_here), jnp.int32)
        for r in range(REQ):
            owner = owner + (logical >= ends[r]).astype(jnp.int32)
        mass = dot(picker, mass_v[h], NT)
        mass = jnp.concatenate([mass[g : g + 1] for g in range(PAGES)], axis=1)
        rope = q3_in[HERE + h // 2][:, 64 * (h % 2) : 64 * (h % 2) + 64]
        latent_query = dot(q3_in[h], key_v[h]).astype(BF16)
        scores = dot(latent_query, flat_v[h, :, :RANK], NT) + dot(rope, flat_v[h, :, RANK:], NT)
        scores = scores * scale
        mine_here = owner == request
        best = jnp.max(jnp.where(mine_here, scores, NEG), axis=1, keepdims=True)
        weights = jnp.where(mine_here, mass * jnp.exp(scores - best), 0.0)
        total = jnp.sum(weights, axis=1, keepdims=True)
        summed = dot(weights.astype(BF16), flat_v[h, :, :RANK])
        stats = stats_of(best, total)
        for half in range(2):
            a_out[2 * h + half, :, 0:256] = summed[:, 256 * half : 256 * half + 256].astype(BF16)
            a_out[2 * h + half, :, 256:384] = stats

    def merged(into):
        def stat(n, first):
            return sum(
                into[n, :, 256 + 16 * s : 256 + 16 * s + 16].astype(F32)[:, 0:1]
                for s in range(first, first + 3)
            )

        bests = [stat(n, 0) for n in range(8)]
        best = functools.reduce(jnp.maximum, bests)
        total = jnp.zeros((REQ, 1), F32)
        latent = jnp.zeros((REQ, 256), F32)
        for n in range(8):
            factor = jnp.exp(bests[n] - best)
            total = total + factor * stat(n, 3)
            latent = latent + factor * into[n, :, 0:256].astype(F32)
        return best, total, latent

    exchange(3, "a", a_out, a_in, True)
    best, total, latent = merged(a_in)
    b_out[:, 0:256] = latent.astype(BF16)
    b_out[:, 256:384] = stats_of(best, total)
    exchange(4, "z", b_out, b_in, False)
    _, total, latent = merged(b_in)
    latent_out = (latent / total).astype(BF16)
    loads[2].wait()
    c_out[...] = dot(latent_out, value_v[a // 2, pl.ds((a % 2) * 256, 256), :])
    exchange(5, "a", c_out, c_in, False)

    loads[3].wait()
    cols = jnp.zeros((REQ, 32), F32)
    for h in range(HERE):
        head_out = (c_in[2 * h] + c_in[2 * h + 1]).astype(BF16)
        cols = cols + dot(head_out, outw_v[:, 128 * h : 128 * h + 128], NT)
    spread = jnp.concatenate([cols] * 4, axis=1)
    lane = lax.broadcasted_iota(jnp.int32, spread.shape, 1)
    d_out[...] = jnp.where(lane // 32 == p % 4, spread, 0.0)
    exchange(6, "x", d_out, d_in, False)
    d2_out[...] = added(d_in, NX).astype(BF16)
    exchange(7, "z", d2_out, d2_in, False)
    for n in range(4):
        d3_out[n] = (d2_in[2 * n].astype(F32) + d2_in[2 * n + 1].astype(F32)).astype(BF16)
    exchange(8, "a", d3_out, d3_in, False)

    tiles = [
        d3_in[2 * (t // 4), t % 4].astype(F32) + d3_in[2 * (t // 4) + 1, t % 4].astype(F32)
        for t in range(16)
    ]
    square = jnp.zeros((REQ, 128), F32)
    for t in range(16):
        attn_ref[:, 128 * t : 128 * t + 128] = tiles[t].astype(BF16)
        square = square + tiles[t] * tiles[t]
    mean = jnp.sum(square, axis=1, keepdims=True) * (1.0 / 2048)
    inverse = lax.rsqrt(mean + NORM_EPS)
    normed = jnp.concatenate(
        [
            (tiles[t] * inverse * gain_ref[:, 128 * t : 128 * t + 128].astype(F32)).astype(BF16)
            for t in range(16)
        ],
        axis=1,
    )

    loads[4].wait()
    logits = dot(normed, router_v[...], NT)
    chance = 1.0 / (1.0 + jnp.exp(-logits))
    expert = lax.broadcasted_iota(jnp.int32, chance.shape, 1)
    request = lax.broadcasted_iota(jnp.int32, chance.shape, 0)
    routed = jnp.zeros(chance.shape, F32)
    for t in range(routes_ref.shape[0]):
        route = jnp.zeros(chance.shape, jnp.int32)
        for r in range(REQ):
            route = jnp.where(request == r, routes_ref[t, r], route)
        routed = jnp.where(route == expert, 1.0, routed)
    chosen = routed * chance
    share = ROUTE_SCALE * chosen / jnp.sum(chosen, axis=1, keepdims=True)
    share_here = jnp.sum(jnp.where(expert == p, share, 0.0), axis=1, keepdims=True)
    loads[5].wait()
    gate = dot(normed, gate_v[...], NT)
    loads[6].wait()
    up = dot(normed, up_v[...], NT)
    expert_hidden = (gate / (1.0 + jnp.exp(-gate)) * up).astype(BF16)
    loads[7].wait()
    for n in range(8):
        e_out[n] = (
            share_here * dot(expert_hidden, down_v[:, 256 * n : 256 * n + 256])
        ).astype(BF16)
    exchange(9, "a", e_out, e_in, True)
    e2_out[...] = added(e_in, 8).astype(BF16)
    exchange(10, "z", e2_out, e2_in, False)
    e3_out[...] = added(e2_in, 8).astype(BF16)
    exchange(11, "x", e3_out, e3_in, False)
    e4_out[...] = added(e3_in, NX).astype(BF16)
    exchange(12, "a", e4_out, e4_in, False)
    feed(len(OFFSETS))
    for n in range(8):
        moe_ref[:, 256 * n : 256 * n + 256] = e4_in[n]

    place = lax.broadcasted_iota(jnp.int32, (BLOCKS, lanes), 0) + p * BLOCKS
    new_mass = jnp.zeros((BLOCKS, KEPT), F32)
    for h in range(HERE):
        owned = (place_ref[h : h + 1, :] == place).astype(F32).astype(BF16)
        new_mass = new_mass + dot(owned, mass_v[h], NT)
    newmass_ref[...] = new_mass.astype(BF16)

    for copy in smalls:
        copy.wait_send()
    for copy in fed:
        copy.wait()

    def put(q, carry):
        block = recv_v[index_s[GROUPS + q, 0]]
        rows_ref[q, :, 0:256] = block[0:64]
        rows_ref[q, :, 256:512] = block[64:128]
        rope = block[128:144].astype(F32)
        rows_ref[q, :, 512:576] = jnp.concatenate(
            [rope[:, 64 * n : 64 * n + 64] for n in range(4)], axis=0
        ).astype(BF16)
        return carry

    lax.fori_loop(0, BLOCKS, put, 0)


def decode(*operands):
    smem = [pl.BlockSpec(memory_space=pltpu.SMEM)] * 3
    small = [pl.BlockSpec(memory_space=pltpu.VMEM)] * 5
    big = [pl.BlockSpec(memory_space=pltpu.HBM)] * 10
    tile = (REQ, 128)
    wide = (REQ, 256)
    stat = (REQ, 384)

    def pair(shape, parts, dtype, scatter):
        return [
            pltpu.VMEM((parts, *shape) if scatter else shape, dtype),
            pltpu.VMEM((parts, *shape), dtype),
        ]

    return pl.pallas_call(
        decode_kernel,
        out_shape=(
            jax.ShapeDtypeStruct((REQ, 2048), BF16),
            jax.ShapeDtypeStruct((REQ, 2048), BF16),
            jax.ShapeDtypeStruct((BLOCKS, KEPT, LATENT), BF16),
            jax.ShapeDtypeStruct((BLOCKS, KEPT), BF16),
        ),
        in_specs=smem + small + big,
        out_specs=(pl.BlockSpec(memory_space=pltpu.VMEM),) * 4,
        scratch_shapes=[
            pltpu.VMEM((HERE, PAGES, LATENT, ROWS), BF16),
            pltpu.VMEM((HERE, KEPT, GROUPS * PAGES), jnp.int32),
            pltpu.VMEM((HERE, KEPT, GROUPS * PAGES), BF16),
            pltpu.VMEM((HERE, QK_NOPE, RANK), BF16),
            pltpu.VMEM((HERE, RANK, 128), BF16),
            pltpu.VMEM((32, 512), BF16),
            pltpu.VMEM((64, 2048), BF16),
            pltpu.VMEM((352, 2048), BF16),
            pltpu.VMEM((352, 2048), BF16),
            pltpu.VMEM((352, 2048), BF16),
            pltpu.VMEM((HERE, PAGES * KEPT, LATENT), BF16),
            pltpu.VMEM((BLOCKS, *PACK), BF16),
            pltpu.VMEM((GROUPS - 1, *PACK), BF16),
            pltpu.VMEM((GROUPS, *PACK), BF16),
            pltpu.VMEM((GROUPS + BLOCKS, 128), jnp.int32),
            pltpu.SMEM((GROUPS + BLOCKS, 128), jnp.int32),
            *pair(tile, 8, F32, True),
            *pair(tile, 8, F32, False),
            *pair(tile, 8, BF16, False),
            *pair(stat, 8, BF16, True),
            *pair(stat, 8, BF16, False),
            *pair(tile, 8, F32, False),
            *pair(tile, NX, F32, False),
            *pair(tile, 8, BF16, False),
            *pair((4, *tile), 8, BF16, False),
            *pair(wide, 8, BF16, True),
            *pair(wide, 8, BF16, False),
            *pair(wide, NX, BF16, False),
            *pair(wide, 8, BF16, False),
            pltpu.SemaphoreType.DMA((9,)),
            pltpu.SemaphoreType.DMA((HERE,)),
            pltpu.SemaphoreType.DMA,
            pltpu.SemaphoreType.DMA((13, 8)),
            pltpu.SemaphoreType.DMA((13, 8)),
            pltpu.SemaphoreType.DMA((GROUPS,)),
            pltpu.SemaphoreType.DMA((GROUPS,)),
        ],
        compiler_params=pltpu.CompilerParams(
            collective_id=0, has_side_effects=True, vmem_limit_bytes=56 << 20
        ),
        name="decode",
    )(*operands)


def shards(
    hidden,
    q_weight,
    key_up,
    value_up_weight,
    out_weight,
    cache,
    page_table,
    seq_pages,
    keep_rows,
    fold_mass,
    new_place,
    norm_gain,
    router,
    routes,
    w_gate,
    w_up,
    w_down,
):
    half = QK_ROPE // 2
    freqs = THETA ** (-2.0 * np.arange(half) / QK_ROPE)
    freqs = jnp.asarray(np.tile(freqs, 4)[None, :], F32)

    def turn(array):
        return jnp.swapaxes(array, -1, -2)

    return decode(
        seq_pages,
        page_table,
        turn(routes),
        hidden,
        q_weight,
        new_place,
        freqs,
        norm_gain.reshape(1, -1),
        turn(cache),
        turn(keep_rows),
        turn(fold_mass),
        key_up,
        value_up_weight,
        turn(out_weight),
        turn(router),
        turn(w_gate),
        turn(w_up),
        w_down,
    )


def solution(mesh):
    in_specs = (
        P(None, "page"),
        P("page", "head"),
        P("head", None, None),
        P("head", None, None),
        P("head", "page"),
        P("head", "page", None, None),
        P("head", "page"),
        P(),
        P("head", None, None),
        P("head", None, None),
        P("head", None),
        P(),
        P(),
        P(),
        P("page", None, "head"),
        P("page", None, "head"),
        P("page", "head", None),
    )
    out_specs = (P(), P(), P(("head", "page"), None, None), P(("head", "page"), None))
    return jax.shard_map(shards, mesh=mesh, in_specs=in_specs, out_specs=out_specs, check_vma=False)
```
